512 devices in a mesh: mod: 512 (over y, z, x, core).
Axes of the slice: x: 4, y: 8, z: 8, core: 2. Of those that a mesh axis runs over, the one named last changes fastest.
Arguments:
- loads: bfloat16 [32, 524288], P(None, 'mod')
- modes: float32 [6, 524288], P(None, 'mod'), may hold values from -0.6 to 0.6
- pinv: bfloat16 [524288, 1024], P('mod')
- schur: bfloat16 [524288, 1024], P('mod')
- coarse_inverse: float32 [3072, 3072], P('mod')
- connectors: int32 [512, 3, 8], P('mod'), may hold values from -1 to 4, as said below
Outputs:
- multipliers: float32 [32, 524288], P(None, 'mod')
The draws below stay inside these ranges and needn't reach their ends.
Inputs may be any that keep to these rules, and one draw needn't show every extreme that they name: connectors[s, 0, b] is 0 for an unused block, or 1, 2, 3, 4 when the block is tied to module s + 1, s - 1, s + 8, s - 8; its partner is the block of that module with the opposite direction (1 with 2, 3 with 4) and the same slot connectors[s, 1, b], which is below 2 (0 on unused blocks). connectors[s, 2, b] is +1 or -1 on used blocks, opposite at the two ends of a connector, and 0 on unused ones. Partners stay within rows of 8 modules along the first kind of direction and within the modules along the second. A module uses at most 2 blocks towards one neighbour, and some module uses 2.
All inputs are finite; a program needn't handle non-finite values.
Results may differ from the reference program's by a relative error of at most 0.0015.
Values sent between devices are 32-bit elements; how exact they have to be, the bound alone decides.
A program may use at most 64 MiB of HBM per device.

```python
import math
import jax
import jax.numpy as jnp
from jax import lax

BLOCK = 128
BLOCKS = 8
NB = 1024
MODES = 6
MAXC = 2
ACROSS = 8
CASES = 32
ITERS = 1
MODULES = 512
COARSE = 3072


def definite_blocks(key):

    def single(one_key):
        jitter_key, scale_key = jax.random.split(one_key)
        jitter = jax.random.normal(jitter_key, (NB, NB), jnp.float32) * (0.25 / math.sqrt(NB))
        scales = jnp.exp(jax.random.uniform(scale_key, (NB,), jnp.float32, 0.0, math.log(2.0)))
        matrix = jnp.eye(NB, dtype=jnp.float32) + jitter + jitter.T
        return scales[:, None] * matrix * scales[None, :]
    stacked = lax.map(single, jax.random.split(key, MODULES))
    return stacked.reshape(MODULES * NB, NB).astype(jnp.bfloat16)


def draw_pinv(key, part):
    return definite_blocks(jax.random.fold_in(key, 11))


def draw_schur(key, part):
    return definite_blocks(jax.random.fold_in(key, 12))


def draw_loads(key, part):
    key_base, key_rows, key_cols = jax.random.split(jax.random.fold_in(key, 21), 3)
    dof_total = MODULES * NB
    baseline = jax.random.normal(key_base, (CASES, dof_total), jnp.float32)
    row_scale = jnp.exp(jax.random.uniform(key_rows, (1, dof_total), jnp.float32, math.log(0.5), math.log(2.0)))
    col_scale = jnp.exp(jax.random.uniform(key_cols, (CASES, 1), jnp.float32, math.log(0.5), math.log(2.0)))
    module_ids = (jnp.arange(dof_total, dtype=jnp.int32) // NB).astype(jnp.float32)
    ramp = 0.5 * (1.0 + 2.0 * module_ids / max(MODULES - 1, 1))
    return (baseline * row_scale * col_scale * ramp[None, :]).astype(jnp.bfloat16)


def draw_coarse_inverse(key, part):
    jitter = jax.random.normal(jax.random.fold_in(key, 31), (COARSE, COARSE), jnp.float32) / math.sqrt(COARSE)
    return 0.6 * (jnp.eye(COARSE, dtype=jnp.float32) + 0.5 * (jitter + jitter.T))


def draw_connectors(key, part):
    keys = jax.random.split(jax.random.fold_in(key, 41), 5)
    module_ids = jnp.arange(MODULES, dtype=jnp.int32)
    scores = jax.random.randint(keys[0], (MODULES, BLOCKS), 0, 1 << 20) * BLOCKS + jnp.arange(BLOCKS, dtype=jnp.int32)[None, :]
    position = jnp.argsort(jnp.argsort(scores, axis=1), axis=1).astype(jnp.int32)
    link_next = jax.random.randint(keys[1], (MODULES,), 0, MAXC + 1)
    link_next = jnp.where(module_ids % ACROSS == ACROSS - 1, 0, link_next).at[0].set(MAXC)
    link_far = jax.random.randint(keys[2], (MODULES,), 0, MAXC + 1)
    link_far = jnp.where(module_ids >= MODULES - ACROSS, 0, link_far).at[0].set(MAXC)
    sign_next = 2 * jax.random.randint(keys[3], (MODULES,), 0, 2) - 1
    sign_far = 2 * jax.random.randint(keys[4], (MODULES,), 0, 2) - 1
    zero_one = jnp.zeros((1,), jnp.int32)
    zero_row = jnp.zeros((ACROSS,), jnp.int32)
    counts = jnp.stack([link_next, jnp.concatenate([zero_one, link_next[:-1]]), link_far, jnp.concatenate([zero_row, link_far[:-ACROSS]])], axis=1)
    orients = jnp.stack([sign_next, -jnp.concatenate([zero_one + 1, sign_next[:-1]]), sign_far, -jnp.concatenate([zero_row + 1, sign_far[:-ACROSS]])], axis=1)
    heading = position // MAXC
    slot_ids = position % MAXC
    live = slot_ids < jnp.take_along_axis(counts, heading, axis=1)
    heading_code = jnp.where(live, heading + 1, 0)
    slot_code = jnp.where(live, slot_ids, 0)
    orient_code = jnp.where(live, jnp.take_along_axis(orients, heading, axis=1), 0)
    return jnp.stack([heading_code, slot_code, orient_code], axis=1).astype(jnp.int32)


def level_of(own_key, shape, pieces, least, high):
    factor_of = 1.0
    for axis_at, blocks in pieces:
        steps = jax.random.uniform(jax.random.fold_in(jax.random.fold_in(own_key, 6), axis_at), (blocks,), jnp.float32, least / len(pieces), high / len(pieces))
        factor_of = factor_of * jnp.repeat(jnp.exp(steps), shape[axis_at] // blocks).reshape((-1,) + (1,) * (len(shape) - 1 - axis_at))
    return factor_of


def normal_values(key, shape, width, bound, shards=(), kind=jnp.bfloat16):
    drawn = width * jax.random.normal(key, shape, jnp.float32)
    if shards:
        drawn = drawn * level_of(key, shape, shards, -0.22, 0.18)
    return jnp.clip(drawn, -bound, bound).astype(kind)


def setup_inputs(seed: int = 0) -> dict:
    arg_keys = jax.random.split(jax.random.key(seed), 7)
    loads = draw_loads(jax.random.fold_in(arg_keys[6], 71), 0)
    modes = normal_values(arg_keys[1], (MODES, MODULES * NB), 0.1, 0.6, ((1, 512),), jnp.float32)
    pinv = draw_pinv(jax.random.fold_in(arg_keys[6], 71), 0)
    schur = draw_schur(jax.random.fold_in(arg_keys[6], 71), 0)
    coarse_inverse = draw_coarse_inverse(jax.random.fold_in(arg_keys[6], 71), 0)
    connectors = draw_connectors(jax.random.fold_in(arg_keys[6], 71), 0)
    return dict(loads=loads, modes=modes, pinv=pinv, schur=schur, coarse_inverse=coarse_inverse, connectors=connectors)


highest = lax.Precision.HIGHEST


def selector_table(connectors):
    headings = connectors[:, 0, :]
    slot_ids = connectors[:, 1, :]
    heading_ids = jnp.arange(4, dtype=jnp.int32)[:, None, None, None] + 1
    slot_range = jnp.arange(MAXC, dtype=jnp.int32)[None, :, None, None]
    return ((headings[None, None] == heading_ids) & (slot_ids[None, None] == slot_range)).astype(jnp.float32)


def shift_modules(values_in, offset):
    module_total = values_in.shape[2]
    if offset > 0:
        padding = jnp.zeros_like(values_in[:, :, :offset])
        return jnp.concatenate([padding, values_in[:, :, :module_total - offset]], axis=2)
    padding = jnp.zeros_like(values_in[:, :, :(-offset)])
    return jnp.concatenate([values_in[:, :, -offset:], padding], axis=2)


def jump_blocks(values_in, orient, selector):
    signed = values_in * orient[None, :, :, None]
    offsets = [1, -1, ACROSS, -ACROSS]
    summed = signed
    for heading in range(4):
        packed = jnp.einsum("knb,cnbe->kcne", selector[heading ^ 1], signed, precision=highest)
        received = shift_modules(packed, -offsets[heading])
        summed = summed + jnp.einsum("knb,kcne->cnbe", selector[heading], received, precision=highest)
    return summed


def reference(loads, modes, pinv, schur, coarse_inverse, connectors):
    case_count = loads.shape[0]
    block_view = (case_count, MODULES, BLOCKS, BLOCK)
    flat_view = (case_count, MODULES, NB)
    orient = connectors[:, 2, :].astype(jnp.float32)
    orient_flat = jnp.repeat(orient, BLOCK, axis=1)[None]
    selector = selector_table(connectors)
    mode_view = modes.reshape(MODES, MODULES, NB)
    pinv_view = pinv.reshape(MODULES, NB, NB)
    schur_view = schur.reshape(MODULES, NB, NB)

    def apply_jump(values_in):
        return jump_blocks(values_in.reshape(block_view), orient, selector).reshape(flat_view)

    def coarse_rhs(values_in):
        return jnp.einsum("ine,cne->nic", mode_view, values_in, precision=highest).reshape(COARSE, case_count)

    def lift(right_side):
        amplitude = jnp.dot(coarse_inverse, right_side, precision=highest).reshape(MODULES, MODES, case_count)
        return jnp.einsum("nic,ine->cne", amplitude, mode_view, precision=highest)

    def project(values_in):
        return values_in - apply_jump(lift(coarse_rhs(orient_flat * values_in)))

    def module_product(left, matrices):
        def single(pair):
            return jnp.dot(pair[0], pair[1], preferred_element_type=jnp.float32)
        result = lax.map(single, (jnp.swapaxes(left, 0, 1), matrices))
        return jnp.swapaxes(result, 0, 1)

    load_values = loads.reshape(flat_view).astype(jnp.float32)
    multipliers = apply_jump(lift(coarse_rhs(load_values)))
    start = (load_values - orient_flat * multipliers).astype(jnp.bfloat16)
    residual = apply_jump(module_product(start, pinv_view))
    rho_before = None
    direction = None
    for iteration in range(ITERS):
        projected = project(residual)
        scaled = (orient_flat * projected).astype(jnp.bfloat16)
        smoothed = module_product(scaled, schur_view)
        rho = jnp.sum(scaled.astype(jnp.float32) * smoothed, axis=(1, 2))
        corrected = project(apply_jump(smoothed))
        if iteration == 0:
            direction = corrected
        else:
            direction = corrected + (rho / rho_before)[:, None, None] * direction
        lifted = (orient_flat * direction).astype(jnp.bfloat16)
        response = module_product(lifted, pinv_view)
        kappa = jnp.sum(lifted.astype(jnp.float32) * response, axis=(1, 2))
        stride = rho / kappa
        multipliers = multipliers + stride[:, None, None] * direction
        if iteration + 1 < ITERS:
            residual = residual - stride[:, None, None] * apply_jump(response)
        rho_before = rho
    return multipliers.reshape(case_count, MODULES * NB)
```

```python
import functools

import jax
import jax.numpy as jnp
from jax import lax
from jax.experimental import pallas as pl
from jax.experimental.pallas import tpu as pltpu
from jax.sharding import PartitionSpec as P

MODES = 6
MAXC = 2
ACROSS = 8
MESH = pl.DeviceIdType.MESH
F32 = jnp.float32
BF16 = jnp.bfloat16


def nt(left, right):
    return lax.dot_general(left, right, (((1,), (1,)), ((), ())), preferred_element_type=F32)


def split(values):
    high = values.astype(BF16)
    rest = values - high.astype(F32)
    middle = rest.astype(BF16)
    low = (rest - middle.astype(F32)).astype(BF16)
    return jnp.concatenate([high, middle, low], axis=0)


def merge(stacked):
    rows = stacked.shape[0] // 3
    return stacked[:rows] + (stacked[rows : 2 * rows] + stacked[2 * rows :])


def kernel(
    loads_h, modes_h, pinv_h, schur_h, cinv_h, conn, out,
    loads_v, modes_v, pinv_v, schur_v, dbuf, lbuf, gbuf, hbuf,
    cbuf, zbuf, pbuf, rbuf, abuf, esend, erecv, msend, mrecv, wsend, wrecv,
    fbuf, fsend, mult, field,
    local_sem, send_sem, recv_sem,
):
    me = lax.axis_index("mod")
    c = lax.rem(me, 8)
    row = lax.div(me, 8)
    z = lax.rem(row, 8)
    y = lax.div(row, 8)
    cs = [row * 8 + lax.rem(c + k, 8) for k in range(1, 8)]
    zs = [y * 64 + lax.rem(z + k, 8) * 8 + c for k in range(1, 8)]
    ys = [lax.rem(y + k, 8) * 64 + z * 8 + c for k in range(1, 8)]
    near = [cs[0], cs[6], lax.rem(me + 8, 512), lax.rem(me + 504, 512)]

    sends = []
    stages = []

    def stage():
        stages.append(None)
        return len(stages) - 1

    def send(src, dst, at, to):
        copy = pltpu.make_async_remote_copy(
            src_ref=src, dst_ref=dst, send_sem=send_sem.at[at], recv_sem=recv_sem.at[at],
            device_id=(to,), device_id_type=MESH,
        )
        copy.start()

    def arrived(ref, at):
        pltpu.make_async_copy(ref, ref, recv_sem.at[at]).wait()
        sends.append((ref, at))

    copies = [
        pltpu.make_async_copy(modes_h, modes_v.at[pl.ds(0, MODES)], local_sem.at[0]),
        pltpu.make_async_copy(loads_h, loads_v, local_sem.at[1]),
        pltpu.make_async_copy(pinv_h, pinv_v, local_sem.at[2]),
        pltpu.make_async_copy(schur_h, schur_v, local_sem.at[3]),
        pltpu.make_async_copy(
            cinv_h.at[:, pl.ds(pl.multiple_of(y * 384, 128), 384)], dbuf.at[y, pl.ds(0, MODES)], local_sem.at[4]
        ),
    ]
    for copy in copies:
        copy.start()
    barrier = pltpu.get_barrier_semaphore()
    for peer in cs + zs + ys + near[2:]:
        pl.semaphore_signal(barrier, inc=1, device_id=(peer,), device_id_type=MESH)

    sub = lax.broadcasted_iota(jnp.int32, (8, 128), 0)
    group = lax.broadcasted_iota(jnp.int32, (8, 128), 1) >> 5
    packing = group == (sub & 3)
    sigma = [conn[0, 2, b].astype(F32) for b in range(8)]
    used = [s * s for s in sigma]
    code = [conn[0, 0, b] * MAXC + conn[0, 1, b] for b in range(8)]
    select = [
        [[jnp.where(code[b] == (h + 1) * MAXC + k, 1.0, 0.0).astype(F32) for b in range(8)] for k in range(MAXC)]
        for h in range(4)
    ]

    def pick(blocks, h, k):
        total = select[h][k][0] * blocks[0]
        for b in range(1, 8):
            total = total + select[h][k][b] * blocks[b]
        return total

    def cols(b):
        return pl.ds(b * 128, 128)

    def gather_start(step, right):
        packed = jnp.where(packing, right, 0.0)
        cbuf[step, c, 0:1, :] = jnp.sum(packed[0:4], axis=0, keepdims=True)
        cbuf[step, c, 1:2, :] = jnp.sum(packed[4:8], axis=0, keepdims=True)

    def gather_row(step):
        at = stage()
        for peer in cs:
            send(cbuf.at[step, c], cbuf.at[step, c], at, peer)
        return at

    def gather_plane(step, at_row):
        arrived(cbuf.at[step, pl.ds(0, 7)], at_row)
        zbuf[step, z] = cbuf[step].reshape(16, 128)
        at = stage()
        for peer in zs:
            send(zbuf.at[step, z], zbuf.at[step, z], at, peer)
        return at

    def partial_solve(step, at_plane):
        arrived(zbuf.at[step, pl.ds(0, 7)], at_plane)
        right = zbuf[step].reshape(128, 128)
        both = jnp.dot(lbuf[...], right, precision=lax.Precision.HIGHEST, preferred_element_type=F32)
        own = jnp.zeros((64, 128), F32)
        wide = lax.broadcasted_iota(jnp.int32, (64, 128), 1) >> 5
        for j in range(4):
            own = own + jnp.where(wide == j, both[64 * j : 64 * j + 64], 0.0)
        pbuf[step] = own.reshape(8, 8, 128)
        at = stage()
        for k, peer in enumerate(ys):
            send(pbuf.at[step, lax.rem(y + k + 1, 8)], rbuf.at[step, y], at, peer)
        rbuf[step, y] = pbuf[step, y]
        return at

    def amplitude(step, at_sum):
        arrived(rbuf.at[step, pl.ds(0, 7)], at_sum)
        total = rbuf[step, 0]
        for k in range(1, 8):
            total = total + rbuf[step, k]
        total = total + pltpu.roll(total, 32, axis=1)
        abuf[step, 0] = total + pltpu.roll(total, 64, axis=1)
        at = stage()
        for h in range(4):
            send(abuf.at[step, 0], abuf.at[step, 1 + (h ^ 1)], at, near[h])
        return at

    def lifted_field(step, at_near):
        arrived(abuf.at[step, pl.ds(0, 4)], at_near)
        values = abuf[step].reshape(40, 128)[:, 0:32]
        return lax.dot_general(
            values, gbuf[...], (((0,), (0,)), ((), ())), precision=lax.Precision.HIGHEST, preferred_element_type=F32
        )

    def contributions(step, which, values):
        four = jnp.concatenate([values] * 4, axis=0)
        parts = merge(nt(hbuf[which], four))
        at = stage()
        for h in range(4):
            esend[step, h] = parts[8 + 8 * h : 16 + 8 * h]
            send(esend.at[step, h], erecv.at[step, h ^ 1], at, near[h])
        return parts[0:8], at

    def right_side(step, own, at):
        arrived(erecv.at[step], at)
        return own + ((erecv[step, 0] + erecv[step, 1]) + (erecv[step, 2] + erecv[step, 3]))

    def swap_blocks(step, values):
        blocks = [values[:, 128 * b : 128 * b + 128] for b in range(8)]
        at = stage()
        for h in range(4):
            for k in range(MAXC):
                wsend[step, h, k] = pick(blocks, h, k)
            send(wsend.at[step, h], wrecv.at[step, h ^ 1], at, near[h])
        for b in range(8):
            field[:, cols(b)] = used[b] * blocks[b]
        return at

    def subtract_partners(step, at):
        arrived(wrecv.at[step], at)
        for b in range(8):
            total = field[:, cols(b)]
            for h in range(4):
                for k in range(MAXC):
                    total = total - select[h][k][b] * wrecv[step, h, k]
            field[:, cols(b)] = total

    def operator(which, matrix):
        hbuf[which] = split(merge(nt(split(jnp.concatenate([gbuf[...], jnp.zeros((8, 1024), F32)], axis=0)), matrix[...])))

    def row_sums(values):
        total = values[:, 0:128]
        for b in range(1, 8):
            total = total + values[:, 128 * b : 128 * b + 128]
        return total

    copies[0].wait()
    copies[1].wait()
    small = lax.broadcasted_iota(jnp.int32, (8, 1024), 0) < MODES
    modes = jnp.where(small, modes_v[...], 0.0)
    loads = loads_v[...]
    stacked = split(jnp.concatenate([modes, jnp.zeros((8, 1024), F32)], axis=0))
    gather_start(0, merge(nt(stacked, jnp.concatenate([loads] * 4, axis=0)))[0:8])
    mode_blocks = [modes[:, 128 * b : 128 * b + 128] for b in range(8)]
    for h in range(4):
        for k in range(MAXC):
            msend[h, k] = pick(mode_blocks, h, k)
    pl.semaphore_wait(barrier, 23)
    at = gather_row(0)
    at_modes = stage()
    for h in range(4):
        send(msend.at[h], mrecv.at[h ^ 1], at_modes, near[h])
    at_d = stage()
    for k, peer in enumerate(ys):
        start = pl.multiple_of(lax.rem(y + k + 1, 8) * 384, 128)
        send(cinv_h.at[:, pl.ds(start, 384)], dbuf.at[y, pl.ds(0, MODES)], at_d, peer)
    at = gather_plane(0, at)

    for b in range(8):
        gbuf[0:8, cols(b)] = used[b] * mode_blocks[b]
    arrived(mrecv, at_modes)
    for h in range(4):
        for b in range(8):
            gbuf[8 + 8 * h : 16 + 8 * h, cols(b)] = -(
                select[h][0][b] * mrecv[h, 0] + select[h][1][b] * mrecv[h, 1]
            )

    copies[4].wait()
    arrived(dbuf.at[pl.ds(0, 7), pl.ds(0, MODES)], at_d)
    small = (lax.broadcasted_iota(jnp.int32, (64, 384), 0) & 7) < MODES
    pieces = split(jnp.where(small, dbuf[...].reshape(64, 384), 0.0))
    wide = lax.broadcasted_iota(jnp.int32, (384, 512), 1)
    mode = (wide & 1) * 4 + (wide >> 7)
    source = ((wide & 127) >> 1) * MODES + mode
    order = (source == lax.broadcasted_iota(jnp.int32, (384, 512), 0)) & (mode < MODES)
    moved = merge(jnp.dot(pieces, jnp.where(order, 1.0, 0.0).astype(BF16), preferred_element_type=F32))
    for j in range(4):
        lbuf[64 * j : 64 * j + 64] = moved[:, 128 * j : 128 * j + 128]

    at = partial_solve(0, at)
    copies[2].wait()
    operator(0, pinv_v)
    at = amplitude(0, at)
    field_value = lifted_field(0, at)
    mult[...] = field_value
    start = (loads.astype(F32) - field_value).astype(BF16)

    own, at = contributions(0, 0, start)
    at_w = swap_blocks(0, jnp.dot(start, pinv_v[...], preferred_element_type=F32))
    gather_start(1, right_side(0, own, at))
    at = gather_row(1)
    copies[3].wait()
    operator(1, schur_v)
    at = gather_plane(1, at)
    subtract_partners(0, at_w)
    at = partial_solve(1, at)
    at = amplitude(1, at)
    scaled = (field[...] - lifted_field(1, at)).astype(BF16)

    own, at = contributions(1, 1, scaled)
    smoothed = jnp.dot(scaled, schur_v[...], preferred_element_type=F32)
    at_w = swap_blocks(1, smoothed)
    gather_start(2, right_side(1, own, at))
    at = gather_row(2)
    rho = row_sums(scaled.astype(F32) * smoothed)
    at = gather_plane(2, at)
    subtract_partners(1, at_w)
    at = partial_solve(2, at)
    at = amplitude(2, at)
    corrected = field[...] - lifted_field(2, at)
    field[...] = corrected
    lifted = corrected.astype(BF16)

    response = jnp.dot(lifted, pinv_v[...], preferred_element_type=F32)
    kappa = row_sums(lifted.astype(F32) * response)
    both = jnp.concatenate([rho, kappa, rho, kappa], axis=0)
    total = lax.dot_general(
        jnp.ones((8, 128), F32), both, (((1,), (1,)), ((), ())),
        precision=lax.Precision.HIGHEST, preferred_element_type=F32,
    )
    for turn, (peers, mine) in enumerate(((cs, c), (zs, z), (ys, y))):
        fbuf[turn, mine] = total
        at = stage()
        for peer in peers:
            send(fbuf.at[turn, mine], fbuf.at[turn, mine], at, peer)
        arrived(fbuf.at[turn, pl.ds(0, 7)], at)
        total = fbuf[turn, 0]
        for k in range(1, 8):
            total = total + fbuf[turn, k]
    spread = jnp.concatenate([total] * 4, axis=0)
    lane = lax.broadcasted_iota(jnp.int32, (32, 128), 1)
    case = lax.broadcasted_iota(jnp.int32, (32, 128), 0)
    rho_all = jnp.sum(jnp.where(lane == case, spread, 0.0), axis=1, keepdims=True)
    kappa_all = jnp.sum(jnp.where(lane == case + 32, spread, 0.0), axis=1, keepdims=True)
    stride = rho_all / kappa_all
    for b in range(8):
        out[:, cols(b)] = sigma[b] * (mult[:, cols(b)] + stride * field[:, cols(b)])
    for ref, at in sends:
        pltpu.make_async_copy(ref, ref, send_sem.at[at]).wait()


def on_device(loads, modes, pinv, schur, coarse_inverse, connectors):
    anywhere = pl.BlockSpec(memory_space=pl.ANY)
    vmem = pltpu.VMEM
    n_stages = 23
    return pl.pallas_call(
        kernel,
        out_shape=jax.ShapeDtypeStruct(loads.shape, F32),
        in_specs=[anywhere] * 5 + [pl.BlockSpec(memory_space=pltpu.SMEM)],
        out_specs=pl.BlockSpec(memory_space=pltpu.VMEM),
        scratch_shapes=[
            vmem((32, 1024), BF16),
            vmem((8, 1024), F32),
            vmem((1024, 1024), BF16),
            vmem((1024, 1024), BF16),
            vmem((8, 8, 384), F32),
            vmem((256, 128), F32),
            vmem((40, 1024), F32),
            vmem((2, 144, 1024), BF16),
            vmem((3, 8, 2, 128), F32),
            vmem((3, 8, 16, 128), F32),
            vmem((3, 8, 8, 128), F32),
            vmem((3, 8, 8, 128), F32),
            vmem((3, 5, 8, 128), F32),
            vmem((2, 4, 8, 128), F32),
            vmem((2, 4, 8, 128), F32),
            vmem((4, MAXC, 8, 128), F32),
            vmem((4, MAXC, 8, 128), F32),
            vmem((2, 4, MAXC, 32, 128), F32),
            vmem((2, 4, MAXC, 32, 128), F32),
            vmem((3, 8, 8, 128), F32),
            vmem((8, 128), F32),
            vmem((32, 1024), F32),
            vmem((32, 1024), F32),
            pltpu.SemaphoreType.DMA((5,)),
            pltpu.SemaphoreType.DMA((n_stages,)),
            pltpu.SemaphoreType.DMA((n_stages,)),
        ],
        compiler_params=pltpu.CompilerParams(
            collective_id=0, has_side_effects=True, vmem_limit_bytes=48 * 1024 * 1024
        ),
    )(loads, modes, pinv, schur, coarse_inverse, connectors)


def solution(mesh):
    in_specs = (
        P(None, "mod"),
        P(None, "mod"),
        P("mod", None),
        P("mod", None),
        P("mod", None),
        P("mod", None, None),
    )
    out_specs = P(None, "mod")
    return jax.shard_map(
        on_device, mesh=mesh, in_specs=in_specs, out_specs=out_specs, check_vma=False
    )
```
